32 devices in a mesh: group: 2 (over y), sky: 4 (over z), depth: 4 (over x, core).
Axes of the slice: x: 2, y: 2, z: 4, core: 2. Of those that a mesh axis runs over, the one named last changes fastest.
Arguments:
- convergence: float32 [512, 32, 128], P(('group', 'sky', 'depth')), parts along dimension 0, may hold values from -6 to 6
- summary_cot: float32 [512, 256], P(('group', 'sky', 'depth')), parts along dimension 0, may hold values from -6 to 6
- stem_w: bfloat16 [16, 64], replicated, may hold values from -1.5 to 1.5
- down_w: bfloat16 [256, 256], replicated, may hold values from -0.375 to 0.375
- block_w: bfloat16 [4, 2, 256, 256], replicated, may hold values from -0.375 to 0.375
- plane_ids: int32 [512, 16], P(('group', 'sky', 'depth')), parts along dimension 0, may hold values from 0 to 63, as said below
- tile_ids: int32 [512, 16], P(('group', 'sky', 'depth')), parts along dimension 0, may hold values from 0 to 31, as said below
- lens_weight: float32 [512, 16], P(('group', 'sky', 'depth')), parts along dimension 0, may hold values from 0.5 to 2
- slab_map: int32 [128], replicated, may hold values from 0 to 63, never falling along the last dimension, each value on 1 to 4 neighbouring positions
Outputs:
- density_adjoint: bfloat16 [256, 1024, 128], P(('group', 'sky'), 'depth'), parts along dimension 0
The draws below stay inside these ranges and needn't reach their ends.
There are 2 independent parts, one for each index of `group`. The reference program is written for one: setup_inputs(seed, part) draws one part's arguments, and reference() takes and returns one part's arrays. A program takes and returns all parts, laid end to end along the dimension named above; an argument that names none is the same for every part. Nothing has to cross between parts.
Inputs may be any that keep to these rules, and one draw needn't show every extreme that they name: `plane_ids`: an owner is a pair (plane slab, tile range): planes l with l // 16 equal and tiles t with t // 8 equal. Of the 256 intersection entries of the 16 patches of one device (aligned blocks of 16 rows), at most 32 fall to one owner; some owner receives exactly 32 from every device's block. `tile_ids`: tile indices within a plane; see plane_ids for the bound per owner. `slab_map`: never falls along z; every plane owns at least one cell.
All inputs are finite; a program needn't handle non-finite values.
Results may differ from the reference program's by a relative error of at most 0.018.
Values may be sent and summed in bfloat16 or wider, within the bound.
A program may use at most 64 MiB of HBM per device.

```python
import math
import jax
import jax.numpy as jnp
import numpy as np
from jax import lax

C1 = 64
C2 = 256
RB = 4
PH = 32
PW = 128
PD = 16
OV = 16
PLANES = 64
TPD = 8
NZ = 128
PATCHES = 256
ITEMS = 256
CAP = 32
PL_DEV = 16
TILES = 32
NX = 128
NY = 1024
N_SKY = 4
N_DEPTH = 4


def intersection_lists(key):
    accelerator_list = N_SKY * N_DEPTH
    heavy_count = ITEMS // (2 * CAP)
    light_count = ITEMS // CAP
    destination_indices = jnp.arange(accelerator_list, dtype=jnp.int32)
    slab_position_index = destination_indices % N_DEPTH
    preferred_choice = jax.random.randint(jax.random.fold_in(key, 7), (), 0, accelerator_list)
    extra_credit = jnp.where(destination_indices == preferred_choice, 1 << 20, 0).astype(jnp.int32)

    def one_block(block_key):
        key_ranking, key_perm, key_plane, key_tile = jax.random.split(block_key, 4)
        rating_total = jax.random.randint(key_ranking, (accelerator_list,), 0, 1024) - 96 * slab_position_index + extra_credit
        rating_total = rating_total * accelerator_list + destination_indices
        ranked = jnp.argsort(-rating_total, stable=True)
        first = jnp.repeat(ranked[:heavy_count], CAP)
        second = jnp.repeat(ranked[heavy_count:heavy_count + light_count], CAP // 2)
        targets = jax.random.permutation(key_perm, jnp.concatenate([first, second]))
        planes = targets % N_DEPTH * PL_DEV + jax.random.randint(key_plane, (ITEMS,), 0, PL_DEV)
        tiles = targets // N_DEPTH * TPD + jax.random.randint(key_tile, (ITEMS,), 0, TPD)
        return (planes, tiles)
    block_keys = jax.random.split(jax.random.fold_in(key, 11), accelerator_list)
    planes, tiles = jax.vmap(one_block)(block_keys)
    return (planes.reshape(PATCHES, OV).astype(jnp.int32), tiles.reshape(PATCHES, OV).astype(jnp.int32))


def draw_plane_ids(key, part):
    return intersection_lists(key)[0]


def draw_tile_ids(key, part):
    return intersection_lists(key)[1]


def block_scale(rng, shape, cuts, smallest, high):
    level, own = 1.0, jax.random.fold_in(rng, 6)
    for axis_at, blocks in cuts:
        steps = jnp.exp(jax.random.uniform(jax.random.fold_in(own, axis_at), (blocks,), jnp.float32, smallest / len(cuts), high / len(cuts)))
        level = level * jnp.repeat(steps, shape[axis_at] // blocks).reshape([-1 if axis == axis_at else 1 for axis in range(len(shape))])
    return level


def profile(amount, total, reach, lean):
    weights = [(1 << 20) // math.isqrt(standing ** lean) + 1 for standing in range(2, amount + 1)]
    rest, given = total - reach - (amount - 1), [1] * (amount - 1)
    while rest > 0:
        candidates = [i for i in range(amount - 1) if given[i] < reach]
        whole, remaining = sum([weights[i] for i in candidates]), rest
        for i in candidates:
            addition = min(reach - given[i], max(1, remaining * weights[i] // whole), rest)
            given[i] = given[i] + addition
            rest = rest - addition
    return np.array([reach] + given)


def ragged(own_key, number_of, total, most, lean):
    if number_of == 2:
        one = jax.random.randint(own_key, (), max(1, total - most), min(most, total - 1) + 1)
        return jnp.stack([one, total - one])
    tallies = jnp.asarray(profile(number_of, total, most, lean), jnp.int32)
    twos = (number_of - 1) // 2
    source_of, receiver = tallies[1:1 + 2 * twos:2], tallies[2:2 + 2 * twos:2]
    room = jnp.minimum(source_of - 1, most - receiver)
    passed = jax.random.randint(jax.random.fold_in(own_key, 1), (twos,), 0, 1 << 20) % (room + 1)
    tallies = tallies.at[1:1 + 2 * twos:2].set(source_of - passed).at[2:2 + 2 * twos:2].set(receiver + passed)
    return tallies[jax.random.permutation(jax.random.fold_in(own_key, 2), number_of)]


def noise(rng, extent, deviation, limit, shards=(), held_as=jnp.bfloat16):
    array = jax.random.normal(rng, extent, jnp.float32) * deviation
    if len(shards) > 0:
        array = block_scale(rng, extent, shards, -0.22, 0.18) * array
    return jnp.clip(array, min=-limit, max=limit).astype(held_as)


def setup_inputs(seed: int = 0, part: int = 0) -> dict:
    seeds = jax.random.split(jax.random.key(seed), 10)
    part_splits = jax.random.split(jax.random.fold_in(seeds[9], part), 10)
    convergence = noise(part_splits[0], (PATCHES, PH, PW), 1.0, 6.0, ((0, 16),), jnp.float32)
    summary_cot = noise(part_splits[1], (PATCHES, C2), 1.0, 6.0, ((0, 16),), jnp.float32)
    stem_w = noise(seeds[2], (16, C1), 16 ** -0.5, 1.5)
    down_w = noise(seeds[3], (4 * C1, C2), (4 * C1) ** -0.5, 0.375)
    block_w = noise(seeds[4], (RB, 2, C2, C2), C2 ** -0.5, 0.375)
    plane_ids = draw_plane_ids(jax.random.fold_in(jax.random.fold_in(seeds[9], part), 71), part)
    tile_ids = draw_tile_ids(jax.random.fold_in(jax.random.fold_in(seeds[9], part), 71), part)
    lens_weight = jnp.clip(jnp.exp(math.log(2.0) - 1.3862944 * jax.random.uniform(part_splits[7], (PATCHES, OV), jnp.float32) ** block_scale(part_splits[7], (PATCHES, OV), ((0, 16),), -0.2, 0.2)), 0.5, 2.0)
    slab_map = jnp.searchsorted(jnp.cumsum(ragged(seeds[8], PLANES, NZ, 4, 1)), jnp.arange(NZ), side="right").astype(jnp.int32)
    return dict(convergence=convergence, summary_cot=summary_cot, stem_w=stem_w, down_w=down_w, block_w=block_w, plane_ids=plane_ids, tile_ids=tile_ids, lens_weight=lens_weight, slab_map=slab_map)


def summarize(maps, stem_w, down_w, block_w):
    patch_count, height, breadth = maps.shape
    chans_low = stem_w.shape[1]
    rounded = maps.astype(jnp.bfloat16)
    blocks_four = rounded.reshape(patch_count, height // 4, 4, breadth // 4, 4)
    stem_in = blocks_four.transpose(2, 4, 0, 1, 3).reshape(16, patch_count * (height // 4) * (breadth // 4))
    stem_out = jax.nn.silu(jnp.dot(stem_w.T, stem_in, preferred_element_type=jnp.float32)).astype(jnp.bfloat16)
    coarse = stem_out.reshape(chans_low, patch_count, height // 8, 2, breadth // 8, 2)
    down_in = coarse.transpose(0, 3, 5, 1, 2, 4).reshape(4 * chans_low, patch_count * (height // 8) * (breadth // 8))
    stream = jax.nn.silu(jnp.dot(down_w.T, down_in, preferred_element_type=jnp.float32))
    for layer in range(block_w.shape[0]):
        inner = jax.nn.silu(jnp.dot(block_w[layer, 0].T, stream.astype(jnp.bfloat16), preferred_element_type=jnp.float32)).astype(jnp.bfloat16)
        stream = stream + jnp.dot(block_w[layer, 1].T, inner, preferred_element_type=jnp.float32)
    pooled = stream.reshape(stream.shape[0], patch_count, -1).sum(axis=2)
    return pooled.T

def reference(convergence, summary_cot, stem_w, down_w, block_w, plane_ids, tile_ids, lens_weight, slab_map):
    accelerator_list = N_SKY * N_DEPTH

    def one_block(pair):
        maps, cotangent = pair
        _, pullback = jax.vjp(lambda values: summarize(values, stem_w, down_w, block_w), maps)
        return pullback(cotangent)[0]
    grads = lax.map(one_block, (convergence.reshape(accelerator_list, PD, PH, PW), summary_cot.reshape(accelerator_list, PD, C2)))
    grads = grads.reshape(PATCHES, PH * PW)
    planes = jnp.zeros((PLANES, TILES, PH * PW), jnp.float32)
    for intersection in range(OV):
        rounded = lax.optimization_barrier((lens_weight[:, intersection][:, None] * grads).astype(jnp.bfloat16))
        planes = planes.at[plane_ids[:, intersection], tile_ids[:, intersection]].add(rounded.astype(jnp.float32))
    planes = planes.reshape(PLANES, N_SKY, TPD, PH, PW).transpose(0, 1, 3, 2, 4).reshape(PLANES, NX, NY)
    thickness = jnp.zeros((PLANES,), jnp.float32).at[slab_map].add(jnp.ones((NZ,), jnp.float32))
    recip = 1.0 / thickness
    pencil = planes[slab_map] * recip[slab_map][:, None, None]
    return pencil.transpose(1, 2, 0).astype(jnp.bfloat16)
```

```python
import jax
import jax.numpy as jnp
from jax import lax
from jax.sharding import PartitionSpec as P

PLANES = 64
TPD = 8


def summarize(maps, stem_w, down_w, block_w):
    patch_count, height, breadth = maps.shape
    chans_low = stem_w.shape[1]
    rounded = maps.astype(jnp.bfloat16)
    blocks_four = rounded.reshape(patch_count, height // 4, 4, breadth // 4, 4)
    stem_in = blocks_four.transpose(2, 4, 0, 1, 3).reshape(
        16, patch_count * (height // 4) * (breadth // 4)
    )
    stem_out = jax.nn.silu(jnp.dot(stem_w.T, stem_in, preferred_element_type=jnp.float32)).astype(
        jnp.bfloat16
    )
    coarse = stem_out.reshape(chans_low, patch_count, height // 8, 2, breadth // 8, 2)
    down_in = coarse.transpose(0, 3, 5, 1, 2, 4).reshape(
        4 * chans_low, patch_count * (height // 8) * (breadth // 8)
    )
    stream = jax.nn.silu(jnp.dot(down_w.T, down_in, preferred_element_type=jnp.float32))
    for layer in range(block_w.shape[0]):
        inner = jax.nn.silu(
            jnp.dot(
                block_w[layer, 0].T, stream.astype(jnp.bfloat16), preferred_element_type=jnp.float32
            )
        ).astype(jnp.bfloat16)
        stream = stream + jnp.dot(block_w[layer, 1].T, inner, preferred_element_type=jnp.float32)
    pooled = stream.reshape(stream.shape[0], patch_count, -1).sum(axis=2)
    return pooled.T


def body_exchange(
    convergence, summary_cot, stem_w, down_w, block_w, plane_ids, tile_ids, lens_weight, slab_map
):
    sky_count = lax.axis_size("sky")
    depth_count = lax.axis_size("depth")
    patch_here, height, breadth = convergence.shape
    pixels = height * breadth
    intersections = plane_ids.shape[1]
    slab_planes = PLANES // depth_count
    target_count = slab_planes * TPD
    _, pullback = jax.vjp(lambda values: summarize(values, stem_w, down_w, block_w), convergence)
    grads = pullback(summary_cot)[0].reshape(patch_here, pixels)
    target_rows = jnp.arange(target_count, dtype=jnp.int32)
    accelerator_list = sky_count * depth_count
    entries = patch_here * intersections
    capacity = max(2, 2 * entries // accelerator_list)
    weighted = (
        (lens_weight[:, :, None] * grads[:, None, :]).astype(jnp.bfloat16).reshape(entries, pixels)
    )
    flat_planes = plane_ids.reshape(-1)
    flat_tiles = tile_ids.reshape(-1)
    owner = flat_tiles // TPD * depth_count + flat_planes // slab_planes
    hits = (owner[:, None] == jnp.arange(accelerator_list, dtype=jnp.int32)[None, :]).astype(
        jnp.int32
    )
    before = jnp.sum((jnp.cumsum(hits, axis=0) - hits) * hits, axis=1)
    slot_index = owner * capacity + before
    local_slot = flat_planes % slab_planes * TPD + flat_tiles % TPD
    outgoing = (
        jnp.zeros((accelerator_list * capacity, pixels), jnp.bfloat16).at[slot_index].set(weighted)
    )
    outgoing = outgoing.reshape(sky_count, depth_count, capacity, pixels)
    out_slots = (
        jnp.full((accelerator_list * capacity,), -1, jnp.int32).at[slot_index].set(local_slot)
    )
    out_slots = out_slots.reshape(sky_count, depth_count, capacity)
    incoming, in_slots = (
        lax.all_to_all(
            lax.all_to_all(outgoing, "sky", split_axis=0, concat_axis=0, tiled=True),
            "depth",
            split_axis=1,
            concat_axis=1,
            tiled=True,
        ),
        lax.all_to_all(
            lax.all_to_all(out_slots, "sky", split_axis=0, concat_axis=0, tiled=True),
            "depth",
            split_axis=1,
            concat_axis=1,
            tiled=True,
        ),
    )
    selector = (in_slots.reshape(-1)[None, :] == target_rows[:, None]).astype(jnp.bfloat16)
    deposit = jnp.dot(selector, incoming.reshape(-1, pixels), preferred_element_type=jnp.float32)
    plane_block = (
        deposit.reshape(slab_planes, TPD, height, breadth)
        .transpose(0, 2, 1, 3)
        .reshape(slab_planes, height, TPD * breadth)
    )
    pencil_planes = lax.all_to_all(
        plane_block.astype(jnp.bfloat16), "depth", split_axis=2, concat_axis=0, tiled=True
    ).astype(plane_block.dtype)
    member = (slab_map[:, None] == jnp.arange(PLANES, dtype=jnp.int32)[None, :]).astype(jnp.float32)
    thickness = jnp.sum(member, axis=0)
    spread = member * (1.0 / thickness)[None, :]
    pencil = jnp.einsum("lxy,zl->xyz", pencil_planes, spread, precision=lax.Precision.HIGHEST)
    return pencil.astype(jnp.bfloat16)


def gradients(convergence, summary_cot, stem_w, down_w, block_w):
    _, pullback = jax.vjp(lambda values: summarize(values, stem_w, down_w, block_w), convergence)
    return pullback(summary_cot)[0]


def body_gather(
    convergence, summary_cot, stem_w, down_w, block_w, plane_ids, tile_ids, lens_weight, slab_map
):
    depth_count = lax.axis_size("depth")
    tiles_here = TPD // depth_count
    first_tile = lax.axis_index("sky") * TPD + lax.axis_index("depth") * tiles_here
    patch_here, height, breadth = convergence.shape
    tile_count = lax.axis_size("sky") * TPD
    code = (plane_ids * tile_count + tile_ids).astype(jnp.float32)
    table = lax.all_gather(
        jnp.concatenate([code, lens_weight], axis=1), ("sky", "depth"), axis=0, tiled=True
    )
    ov = plane_ids.shape[1]
    codes, weights = table[:, :ov].astype(jnp.int32), table[:, ov:]
    thickness = jnp.sum((slab_map[:, None] == slab_map[None, :]).astype(jnp.float32), axis=0)
    wanted = (
        slab_map[None, :] * tile_count
        + first_tile
        + jnp.arange(tiles_here, dtype=jnp.int32)[:, None]
    )
    mixing = jnp.sum(
        jnp.where(codes[:, :, None, None] == wanted[None, None], weights[:, :, None, None], 0.0),
        axis=1,
    )
    mixing = (mixing * (1.0 / thickness)[None, None, :]).astype(jnp.bfloat16)
    grads = gradients(convergence, summary_cot, stem_w, down_w, block_w)
    everyone = lax.all_gather(
        grads.astype(jnp.bfloat16), ("sky", "depth"), axis=0, tiled=True
    )
    pencil = jnp.einsum("pxy,ptz->xtyz", everyone, mixing, preferred_element_type=jnp.float32)
    return pencil.astype(jnp.bfloat16).reshape(height, tiles_here * breadth, -1)


def body(convergence, summary_cot, stem_w, down_w, block_w, plane_ids, *rest):
    group = lax.axis_size("sky") * lax.axis_size("depth")
    gathered = group * convergence.shape[0]
    exchanged = 2 * plane_ids.size
    form = body_gather if gathered <= exchanged else body_exchange
    return form(convergence, summary_cot, stem_w, down_w, block_w, plane_ids, *rest)


def solution(mesh):
    placed = (
        P(("group", "sky", "depth"), None, None),
        P(("group", "sky", "depth"), None),
        P(),
        P(),
        P(),
        P(("group", "sky", "depth"), None),
        P(("group", "sky", "depth"), None),
        P(("group", "sky", "depth"), None),
        P(),
    )
    return jax.shard_map(
        body,
        mesh=mesh,
        in_specs=placed,
        out_specs=P(("group", "sky"), "depth", None),
        check_vma=False,
    )
```

```python
import functools

import jax
import jax.numpy as jnp
from jax import lax
from jax.experimental import pallas as pl
from jax.experimental.pallas import tpu as pltpu
from jax.sharding import PartitionSpec as P

PLANES = 64
TPD = 8


def summarize(maps, stem_w, down_w, block_w):
    patch_count, height, breadth = maps.shape
    chans_low = stem_w.shape[1]
    rounded = maps.astype(jnp.bfloat16)
    blocks_four = rounded.reshape(patch_count, height // 4, 4, breadth // 4, 4)
    stem_in = blocks_four.transpose(2, 4, 0, 1, 3).reshape(
        16, patch_count * (height // 4) * (breadth // 4)
    )
    stem_out = jax.nn.silu(jnp.dot(stem_w.T, stem_in, preferred_element_type=jnp.float32)).astype(
        jnp.bfloat16
    )
    coarse = stem_out.reshape(chans_low, patch_count, height // 8, 2, breadth // 8, 2)
    down_in = coarse.transpose(0, 3, 5, 1, 2, 4).reshape(
        4 * chans_low, patch_count * (height // 8) * (breadth // 8)
    )
    stream = jax.nn.silu(jnp.dot(down_w.T, down_in, preferred_element_type=jnp.float32))
    for layer in range(block_w.shape[0]):
        inner = jax.nn.silu(
            jnp.dot(
                block_w[layer, 0].T, stream.astype(jnp.bfloat16), preferred_element_type=jnp.float32
            )
        ).astype(jnp.bfloat16)
        stream = stream + jnp.dot(block_w[layer, 1].T, inner, preferred_element_type=jnp.float32)
    pooled = stream.reshape(stream.shape[0], patch_count, -1).sum(axis=2)
    return pooled.T


def body_exchange(
    convergence, summary_cot, stem_w, down_w, block_w, plane_ids, tile_ids, lens_weight, slab_map
):
    sky_count = lax.axis_size("sky")
    depth_count = lax.axis_size("depth")
    patch_here, height, breadth = convergence.shape
    pixels = height * breadth
    intersections = plane_ids.shape[1]
    slab_planes = PLANES // depth_count
    target_count = slab_planes * TPD
    _, pullback = jax.vjp(lambda values: summarize(values, stem_w, down_w, block_w), convergence)
    grads = pullback(summary_cot)[0].reshape(patch_here, pixels)
    target_rows = jnp.arange(target_count, dtype=jnp.int32)
    accelerator_list = sky_count * depth_count
    entries = patch_here * intersections
    capacity = max(2, 2 * entries // accelerator_list)
    weighted = (
        (lens_weight[:, :, None] * grads[:, None, :]).astype(jnp.bfloat16).reshape(entries, pixels)
    )
    flat_planes = plane_ids.reshape(-1)
    flat_tiles = tile_ids.reshape(-1)
    owner = flat_tiles // TPD * depth_count + flat_planes // slab_planes
    hits = (owner[:, None] == jnp.arange(accelerator_list, dtype=jnp.int32)[None, :]).astype(
        jnp.int32
    )
    before = jnp.sum((jnp.cumsum(hits, axis=0) - hits) * hits, axis=1)
    slot_index = owner * capacity + before
    local_slot = flat_planes % slab_planes * TPD + flat_tiles % TPD
    outgoing = (
        jnp.zeros((accelerator_list * capacity, pixels), jnp.bfloat16).at[slot_index].set(weighted)
    )
    outgoing = outgoing.reshape(sky_count, depth_count, capacity, pixels)
    out_slots = (
        jnp.full((accelerator_list * capacity,), -1, jnp.int32).at[slot_index].set(local_slot)
    )
    out_slots = out_slots.reshape(sky_count, depth_count, capacity)
    incoming, in_slots = (
        lax.all_to_all(
            lax.all_to_all(outgoing, "sky", split_axis=0, concat_axis=0, tiled=True),
            "depth",
            split_axis=1,
            concat_axis=1,
            tiled=True,
        ),
        lax.all_to_all(
            lax.all_to_all(out_slots, "sky", split_axis=0, concat_axis=0, tiled=True),
            "depth",
            split_axis=1,
            concat_axis=1,
            tiled=True,
        ),
    )
    selector = (in_slots.reshape(-1)[None, :] == target_rows[:, None]).astype(jnp.bfloat16)
    deposit = jnp.dot(selector, incoming.reshape(-1, pixels), preferred_element_type=jnp.float32)
    plane_block = (
        deposit.reshape(slab_planes, TPD, height, breadth)
        .transpose(0, 2, 1, 3)
        .reshape(slab_planes, height, TPD * breadth)
    )
    pencil_planes = lax.all_to_all(
        plane_block.astype(jnp.bfloat16), "depth", split_axis=2, concat_axis=0, tiled=True
    ).astype(plane_block.dtype)
    member = (slab_map[:, None] == jnp.arange(PLANES, dtype=jnp.int32)[None, :]).astype(jnp.float32)
    thickness = jnp.sum(member, axis=0)
    spread = member * (1.0 / thickness)[None, :]
    pencil = jnp.einsum("lxy,zl->xyz", pencil_planes, spread, precision=lax.Precision.HIGHEST)
    return pencil.astype(jnp.bfloat16)


MESH = pl.DeviceIdType.MESH


def sigmoid(v):
    return 0.5 * jnp.tanh(0.5 * v) + 0.5


def silu_pair(v):
    gate = sigmoid(v)
    value = v * gate
    return value, gate + value * (1.0 - gate)


def dot(a, b):
    return jnp.dot(a, b, preferred_element_type=jnp.float32)


def dot_t(a, b):
    return lax.dot_general(a, b, (((1,), (1,)), ((), ())), preferred_element_type=jnp.float32)


def pencil_kernel(
    sizes,
    conv,
    cot,
    stem_w,
    down_w,
    block_w,
    planes,
    tiles,
    lens,
    slab,
    out,
    grads,
    table,
    taps,
    mixing,
    send_sem,
    recv_sem,
    table_send,
    table_recv,
):
    sky_count, depth_count, tile_count = sizes
    bf = jnp.bfloat16
    patch, height, width = conv.shape
    low, wide = stem_w.shape[1], down_w.shape[0]
    chunks, across = height // 8, width // 8
    ov = planes.shape[1]
    tiles_here = TPD // depth_count
    group = sky_count * depth_count
    sky, depth = lax.axis_index("sky"), lax.axis_index("depth")
    core = lax.rem(depth, 2)
    partner = depth + 1 - 2 * core
    columns = depth_count // 2
    me = sky * depth_count + depth

    def shifted(by_sky, by_depth):
        return lax.rem(sky + by_sky, sky_count), lax.rem(depth + by_depth, depth_count)

    barrier = pltpu.get_barrier_semaphore()
    for step in range(1, group):
        to_sky, to_depth = shifted(step // depth_count, step % depth_count)
        pl.semaphore_signal(
            barrier, inc=1, device_id={"sky": to_sky, "depth": to_depth}, device_id_type=MESH
        )

    table[me, :, 0:ov] = (planes[...] * tile_count + tiles[...]).astype(jnp.float32)
    table[me, :, ov : 2 * ov] = lens[...]

    row = lax.broadcasted_iota(jnp.int32, (8 * width, patch), 0)
    tap = ((row >> (width.bit_length() - 1)) & 3) * 4 + (row & 3)
    pick = (tap == lax.broadcasted_iota(jnp.int32, (8 * width, patch), 1)).astype(bf)
    widen = (
        lax.broadcasted_iota(jnp.int32, (low, wide), 1) >> 2
        == lax.broadcasted_iota(jnp.int32, (low, wide), 0)
    ).astype(bf)
    spread = dot(pick, dot(stem_w[...], widen).astype(bf))
    row = lax.broadcasted_iota(jnp.int32, (8 * width, wide), 0)
    lane = lax.broadcasted_iota(jnp.int32, (8 * width, wide), 1)
    row_half = row >> (width.bit_length() + 1)
    same = (row_half == ((lane >> 1) & 1)) & (((row >> 2) & 1) == (lane & 1))
    taps[...] = jnp.where(same, spread, 0.0).astype(bf)

    pl.semaphore_wait(barrier, group - 1)

    def table_copy(step):
        to_sky, to_depth = shifted(step // depth_count, step % depth_count)
        return pltpu.make_async_remote_copy(
            src_ref=table.at[me],
            dst_ref=table.at[me],
            send_sem=table_send.at[step],
            recv_sem=table_recv.at[me],
            device_id={"sky": to_sky, "depth": to_depth},
            device_id_type=MESH,
        )

    for step in range(1, group):
        table_copy(step).start()

    positions = across * patch
    lane_group = lax.broadcasted_iota(jnp.int32, (patch, width), 1) >> 3

    def compute(q):
        streams = []
        for r in range(8):
            rows = conv[:, pl.ds(q * 8 + r, 1), :].reshape(patch, width)
            streams.append(
                jnp.concatenate(
                    [jnp.where(lane_group == b, rows, 0.0).astype(bf) for b in range(across)],
                    axis=0,
                )
            )
        stem_in = jnp.concatenate(streams, axis=1)
        stem, stem_slope = silu_pair(dot(stem_in, taps[...]))
        stream, down_slope = silu_pair(dot(stem.astype(bf), down_w[...]))
        slopes = []
        for layer in range(block_w.shape[0]):
            inner, slope = silu_pair(dot(stream.astype(bf), block_w[layer, 0]))
            slopes.append(slope)
            if layer + 1 < block_w.shape[0]:
                stream = stream + dot(inner.astype(bf), block_w[layer, 1])
        flow = jnp.concatenate([cot[...]] * across, axis=0)
        for layer in reversed(range(block_w.shape[0])):
            inner = dot_t(flow.astype(bf), block_w[layer, 1]).astype(bf).astype(jnp.float32)
            inner = (inner * slopes[layer]).astype(bf)
            flow = flow + dot_t(inner, block_w[layer, 0]).astype(bf).astype(jnp.float32)
        flow = dot_t((flow * down_slope).astype(bf), down_w[...]).astype(bf).astype(jnp.float32)
        flow = (flow * stem_slope).astype(bf)
        for r in range(8):
            back = dot_t(flow, taps[pl.ds(r * width, width), :])
            total = jnp.zeros((patch, width), jnp.float32)
            for b in range(across):
                total = jnp.where(lane_group == b, back[b * patch : (b + 1) * patch], total)
            grads[me, q * 8 + r] = total.astype(bf)

    def block_copy(q, source, to_sky, to_depth, slot):
        block = grads.at[source, pl.ds(q * 8, 8)]
        return pltpu.make_async_remote_copy(
            src_ref=block,
            dst_ref=block,
            send_sem=send_sem.at[slot, q],
            recv_sem=recv_sem.at[source, q],
            device_id={"sky": to_sky, "depth": to_depth},
            device_id_type=MESH,
        )

    def index(a, b):
        return a * depth_count + b

    def plan():
        own, relay, last = [], [], []
        slot = 0
        for step in range(1, sky_count):
            own.append((me, lax.rem(sky + step, sky_count), depth, slot))
            slot += 1
        for step in range(1, columns):
            own.append((me, sky, lax.rem(depth + 2 * step, depth_count), slot))
            slot += 1
        own.append((me, sky, partner, slot))
        slot += 1
        for step in range(1, sky_count):
            source = index(lax.rem(sky + step, sky_count), depth)
            sends = []
            for other in range(1, columns):
                sends.append((source, sky, lax.rem(depth + 2 * other, depth_count), slot))
                slot += 1
            sends.append((source, sky, partner, slot))
            slot += 1
            relay.append((source, sends))
        for step in range(sky_count):
            for other in range(1, columns):
                source = index(
                    lax.rem(sky + step, sky_count), lax.rem(depth + 2 * other, depth_count)
                )
                last.append((source, [(source, sky, partner, slot)]))
                slot += 1
        final = [
            index(lax.rem(sky + step, sky_count), lax.rem(partner + 2 * other, depth_count))
            for step in range(sky_count)
            for other in range(columns)
        ]
        return own, relay, last, final

    own, relay, last, final = plan()

    def arrived(q, source):
        block_copy(q, source, sky, partner, 0).wait_recv()

    def forward(q, items):
        for source, sends in items:
            arrived(q, source)
            for send in sends:
                block_copy(q, *send).start()

    def mix_tables():
        for step in range(1, group):
            a, b = shifted(step // depth_count, step % depth_count)
            pltpu.make_async_remote_copy(
                src_ref=table.at[me],
                dst_ref=table.at[index(a, b)],
                send_sem=table_send.at[step],
                recv_sem=table_recv.at[index(a, b)],
                device_id={"sky": a, "depth": b},
                device_id_type=MESH,
            ).wait_recv()
        first_tile = (sky * TPD + depth * tiles_here).astype(jnp.float32)
        cells = slab[...].astype(jnp.float32)
        cell_count = cells.shape[1]
        square = jnp.broadcast_to(cells, (cell_count, cell_count))
        thickness = jnp.sum((square == square.T).astype(jnp.float32), axis=0, keepdims=True)
        wanted = jnp.concatenate(
            [cells * float(tile_count) + first_tile + float(t) for t in range(tiles_here)], axis=1
        )
        inverse = jnp.concatenate([1.0 / thickness] * tiles_here, axis=1)

        @pl.loop(0, group)
        def _(device):
            entries = table[device]
            total = jnp.zeros((patch, wanted.shape[1]), jnp.float32)
            for k in range(ov):
                hit = entries[:, k : k + 1] == wanted
                total = total + jnp.where(hit, entries[:, ov + k : ov + k + 1], 0.0)
            mixing[device] = (total * inverse).astype(bf)

    def deposit(q):
        weights = mixing[...].reshape(group * patch, -1)
        cell_count = slab.shape[1]
        for r in range(8):
            rows = grads[:, pl.ds(q * 8 + r, 1)].reshape(group * patch, width)
            made = lax.dot_general(
                rows, weights, (((0,), (0,)), ((), ())), preferred_element_type=jnp.float32
            ).astype(bf)
            for t in range(tiles_here):
                out[q * 8 + r, t * width : (t + 1) * width, :] = made[
                    :, t * cell_count : (t + 1) * cell_count
                ]

    def step_body(k, carry):
        @pl.when(k < chunks)
        def _():
            compute(k)
            for send in own:
                block_copy(k, *send).start()

        @pl.when((k >= 1) & (k < chunks + 1))
        def _():
            forward(k - 1, relay)

        @pl.when((k >= 2) & (k < chunks + 2))
        def _():
            forward(k - 2, last)

        @pl.when(k == 2)
        def _():
            mix_tables()

        @pl.when(k >= 3)
        def _():
            for source in final:
                arrived(k - 3, source)
            deposit(k - 3)

        return carry

    lax.fori_loop(0, chunks + 3, step_body, 0)

    def drain(q, carry):
        for send in own:
            block_copy(q, *send).wait_send()
        for source, sends in relay + last:
            for send in sends:
                block_copy(q, *send).wait_send()
        return carry

    lax.fori_loop(0, chunks, drain, 0)
    for step in range(1, group):
        table_copy(step).wait_send()


def body_gather(
    convergence, summary_cot, stem_w, down_w, block_w, plane_ids, tile_ids, lens_weight, slab_map
):
    sky_count, depth_count = lax.axis_size("sky"), lax.axis_size("depth")
    group = sky_count * depth_count
    patch, height, width = convergence.shape
    tiles_here = TPD // depth_count
    cells = slab_map.shape[0]
    vmem = pl.BlockSpec(memory_space=pltpu.VMEM)
    chunks = height // 8
    return pl.pallas_call(
        functools.partial(pencil_kernel, (sky_count, depth_count, sky_count * TPD)),
        out_shape=jax.ShapeDtypeStruct((height, tiles_here * width, cells), jnp.bfloat16),
        in_specs=[vmem] * 9,
        out_specs=vmem,
        scratch_shapes=[
            pltpu.VMEM((group, height, patch, width), jnp.bfloat16),
            pltpu.VMEM((group, patch, 128), jnp.float32),
            pltpu.VMEM((8 * width, down_w.shape[0]), jnp.bfloat16),
            pltpu.VMEM((group, patch, tiles_here * cells), jnp.bfloat16),
            pltpu.SemaphoreType.DMA((group, chunks)),
            pltpu.SemaphoreType.DMA((group, chunks)),
            pltpu.SemaphoreType.DMA((group,)),
            pltpu.SemaphoreType.DMA((group,)),
        ],
        compiler_params=pltpu.CompilerParams(
            collective_id=0, has_side_effects=True, vmem_limit_bytes=50 * 2**20
        ),
        name="pencil",
    )(
        convergence,
        summary_cot,
        stem_w,
        down_w,
        block_w,
        plane_ids,
        tile_ids,
        lens_weight,
        slab_map.reshape(1, cells),
    )


def body(convergence, summary_cot, stem_w, down_w, block_w, plane_ids, *rest):
    group = lax.axis_size("sky") * lax.axis_size("depth")
    gathered = group * convergence.shape[0]
    exchanged = 2 * plane_ids.size
    form = body_gather if gathered <= exchanged else body_exchange
    return form(convergence, summary_cot, stem_w, down_w, block_w, plane_ids, *rest)


def solution(mesh):
    placed = (
        P(("group", "sky", "depth"), None, None),
        P(("group", "sky", "depth"), None),
        P(),
        P(),
        P(),
        P(("group", "sky", "depth"), None),
        P(("group", "sky", "depth"), None),
        P(("group", "sky", "depth"), None),
        P(),
    )
    return jax.shard_map(
        body,
        mesh=mesh,
        in_specs=placed,
        out_specs=P(("group", "sky"), "depth", None),
        check_vma=False,
    )
```

```python
import functools

import jax
import jax.numpy as jnp
from jax import lax
from jax.experimental import pallas as pl
from jax.experimental.pallas import tpu as pltpu
from jax.sharding import PartitionSpec as P

PLANES = 64
TPD = 8


def summarize(maps, stem_w, down_w, block_w):
    patch_count, height, breadth = maps.shape
    chans_low = stem_w.shape[1]
    rounded = maps.astype(jnp.bfloat16)
    blocks_four = rounded.reshape(patch_count, height // 4, 4, breadth // 4, 4)
    stem_in = blocks_four.transpose(2, 4, 0, 1, 3).reshape(
        16, patch_count * (height // 4) * (breadth // 4)
    )
    stem_out = jax.nn.silu(jnp.dot(stem_w.T, stem_in, preferred_element_type=jnp.float32)).astype(
        jnp.bfloat16
    )
    coarse = stem_out.reshape(chans_low, patch_count, height // 8, 2, breadth // 8, 2)
    down_in = coarse.transpose(0, 3, 5, 1, 2, 4).reshape(
        4 * chans_low, patch_count * (height // 8) * (breadth // 8)
    )
    stream = jax.nn.silu(jnp.dot(down_w.T, down_in, preferred_element_type=jnp.float32))
    for layer in range(block_w.shape[0]):
        inner = jax.nn.silu(
            jnp.dot(
                block_w[layer, 0].T, stream.astype(jnp.bfloat16), preferred_element_type=jnp.float32
            )
        ).astype(jnp.bfloat16)
        stream = stream + jnp.dot(block_w[layer, 1].T, inner, preferred_element_type=jnp.float32)
    pooled = stream.reshape(stream.shape[0], patch_count, -1).sum(axis=2)
    return pooled.T


def body_exchange(
    convergence, summary_cot, stem_w, down_w, block_w, plane_ids, tile_ids, lens_weight, slab_map
):
    sky_count = lax.axis_size("sky")
    depth_count = lax.axis_size("depth")
    patch_here, height, breadth = convergence.shape
    pixels = height * breadth
    intersections = plane_ids.shape[1]
    slab_planes = PLANES // depth_count
    target_count = slab_planes * TPD
    _, pullback = jax.vjp(lambda values: summarize(values, stem_w, down_w, block_w), convergence)
    grads = pullback(summary_cot)[0].reshape(patch_here, pixels)
    target_rows = jnp.arange(target_count, dtype=jnp.int32)
    accelerator_list = sky_count * depth_count
    entries = patch_here * intersections
    capacity = max(2, 2 * entries // accelerator_list)
    weighted = (
        (lens_weight[:, :, None] * grads[:, None, :]).astype(jnp.bfloat16).reshape(entries, pixels)
    )
    flat_planes = plane_ids.reshape(-1)
    flat_tiles = tile_ids.reshape(-1)
    owner = flat_tiles // TPD * depth_count + flat_planes // slab_planes
    hits = (owner[:, None] == jnp.arange(accelerator_list, dtype=jnp.int32)[None, :]).astype(
        jnp.int32
    )
    before = jnp.sum((jnp.cumsum(hits, axis=0) - hits) * hits, axis=1)
    slot_index = owner * capacity + before
    local_slot = flat_planes % slab_planes * TPD + flat_tiles % TPD
    outgoing = (
        jnp.zeros((accelerator_list * capacity, pixels), jnp.bfloat16).at[slot_index].set(weighted)
    )
    outgoing = outgoing.reshape(sky_count, depth_count, capacity, pixels)
    out_slots = (
        jnp.full((accelerator_list * capacity,), -1, jnp.int32).at[slot_index].set(local_slot)
    )
    out_slots = out_slots.reshape(sky_count, depth_count, capacity)
    incoming, in_slots = (
        lax.all_to_all(
            lax.all_to_all(outgoing, "sky", split_axis=0, concat_axis=0, tiled=True),
            "depth",
            split_axis=1,
            concat_axis=1,
            tiled=True,
        ),
        lax.all_to_all(
            lax.all_to_all(out_slots, "sky", split_axis=0, concat_axis=0, tiled=True),
            "depth",
            split_axis=1,
            concat_axis=1,
            tiled=True,
        ),
    )
    selector = (in_slots.reshape(-1)[None, :] == target_rows[:, None]).astype(jnp.bfloat16)
    deposit = jnp.dot(selector, incoming.reshape(-1, pixels), preferred_element_type=jnp.float32)
    plane_block = (
        deposit.reshape(slab_planes, TPD, height, breadth)
        .transpose(0, 2, 1, 3)
        .reshape(slab_planes, height, TPD * breadth)
    )
    pencil_planes = lax.all_to_all(
        plane_block.astype(jnp.bfloat16), "depth", split_axis=2, concat_axis=0, tiled=True
    ).astype(plane_block.dtype)
    member = (slab_map[:, None] == jnp.arange(PLANES, dtype=jnp.int32)[None, :]).astype(jnp.float32)
    thickness = jnp.sum(member, axis=0)
    spread = member * (1.0 / thickness)[None, :]
    pencil = jnp.einsum("lxy,zl->xyz", pencil_planes, spread, precision=lax.Precision.HIGHEST)
    return pencil.astype(jnp.bfloat16)


MESH = pl.DeviceIdType.MESH


def sigmoid(v):
    return 0.5 * jnp.tanh(0.5 * v) + 0.5


def silu_pair(v):
    gate = sigmoid(v)
    value = v * gate
    return value, gate + value * (1.0 - gate)


def dot(a, b):
    return jnp.dot(a, b, preferred_element_type=jnp.float32)


def dot_t(a, b):
    return lax.dot_general(a, b, (((1,), (1,)), ((), ())), preferred_element_type=jnp.float32)


def pencil_kernel(
    sizes,
    *refs,
):
    inputs, (out, *held), rest = refs[:9], refs[9:19], refs[19:]
    load_sem, rest = rest[0], rest[1:]
    loads = [
        pltpu.make_async_copy(source, target, load_sem.at[i])
        for i, (source, target) in enumerate(zip(inputs, held))
    ]
    for i in (5, 6, 7, 2, 0, 3, 4, 1, 8):
        loads[i].start()
    pencil_steps(sizes, loads, *held, out, *rest)


def pencil_steps(
    sizes,
    loads,
    conv,
    cot,
    stem_w,
    down_w,
    block_w,
    planes,
    tiles,
    lens,
    slab,
    out,
    grads,
    table,
    taps,
    mixing,
    send_sem,
    recv_sem,
    table_send,
    table_recv,
):
    sky_count, depth_count, tile_count = sizes
    bf = jnp.bfloat16
    patch, height, width = conv.shape
    low, wide = stem_w.shape[1], down_w.shape[0]
    chunks, across = height // 8, width // 8
    ov = planes.shape[1]
    tiles_here = TPD // depth_count
    group = sky_count * depth_count
    sky, depth = lax.axis_index("sky"), lax.axis_index("depth")
    core = lax.rem(depth, 2)
    partner = depth + 1 - 2 * core
    columns = depth_count // 2
    me = sky * depth_count + depth

    def shifted(by_sky, by_depth):
        return lax.rem(sky + by_sky, sky_count), lax.rem(depth + by_depth, depth_count)

    barrier = pltpu.get_barrier_semaphore()
    for step in range(1, group):
        to_sky, to_depth = shifted(step // depth_count, step % depth_count)
        pl.semaphore_signal(
            barrier, inc=1, device_id={"sky": to_sky, "depth": to_depth}, device_id_type=MESH
        )

    for i in (5, 6, 7):
        loads[i].wait()
    table[me, :, 0:ov] = (planes[...] * tile_count + tiles[...]).astype(jnp.float32)
    table[me, :, ov : 2 * ov] = lens[...]

    loads[2].wait()
    row = lax.broadcasted_iota(jnp.int32, (8 * width, patch), 0)
    tap = ((row >> (width.bit_length() - 1)) & 3) * 4 + (row & 3)
    pick = (tap == lax.broadcasted_iota(jnp.int32, (8 * width, patch), 1)).astype(bf)
    widen = (
        lax.broadcasted_iota(jnp.int32, (low, wide), 1) >> 2
        == lax.broadcasted_iota(jnp.int32, (low, wide), 0)
    ).astype(bf)
    spread = dot(pick, dot(stem_w[...], widen).astype(bf))
    row = lax.broadcasted_iota(jnp.int32, (8 * width, wide), 0)
    lane = lax.broadcasted_iota(jnp.int32, (8 * width, wide), 1)
    row_half = row >> (width.bit_length() + 1)
    same = (row_half == ((lane >> 1) & 1)) & (((row >> 2) & 1) == (lane & 1))
    taps[...] = jnp.where(same, spread, 0.0).astype(bf)

    pl.semaphore_wait(barrier, group - 1)

    def table_copy(step):
        to_sky, to_depth = shifted(step // depth_count, step % depth_count)
        return pltpu.make_async_remote_copy(
            src_ref=table.at[me],
            dst_ref=table.at[me],
            send_sem=table_send.at[step],
            recv_sem=table_recv.at[me],
            device_id={"sky": to_sky, "depth": to_depth},
            device_id_type=MESH,
        )

    for step in range(1, group):
        table_copy(step).start()

    for i in (0, 3, 4, 1, 8):
        loads[i].wait()
    lane_group = lax.broadcasted_iota(jnp.int32, (patch, width), 1) >> 3

    def compute(q):
        streams = []
        for r in range(8):
            rows = conv[:, pl.ds(q * 8 + r, 1), :].reshape(patch, width)
            streams.append(
                jnp.concatenate(
                    [jnp.where(lane_group == b, rows, 0.0).astype(bf) for b in range(across)],
                    axis=0,
                )
            )
        stem_in = jnp.concatenate(streams, axis=1)
        stem, stem_slope = silu_pair(dot(stem_in, taps[...]))
        stream, down_slope = silu_pair(dot(stem.astype(bf), down_w[...]))
        slopes = []
        for layer in range(block_w.shape[0]):
            inner, slope = silu_pair(dot(stream.astype(bf), block_w[layer, 0]))
            slopes.append(slope)
            if layer + 1 < block_w.shape[0]:
                stream = stream + dot(inner.astype(bf), block_w[layer, 1])
        flow = jnp.concatenate([cot[...]] * across, axis=0)
        for layer in reversed(range(block_w.shape[0])):
            inner = dot_t(flow.astype(bf), block_w[layer, 1]).astype(bf).astype(jnp.float32)
            inner = (inner * slopes[layer]).astype(bf)
            flow = flow + dot_t(inner, block_w[layer, 0]).astype(bf).astype(jnp.float32)
        flow = dot_t((flow * down_slope).astype(bf), down_w[...]).astype(bf).astype(jnp.float32)
        flow = (flow * stem_slope).astype(bf)
        for r in range(8):
            back = dot_t(flow, taps[pl.ds(r * width, width), :])
            total = jnp.zeros((patch, width), jnp.float32)
            for b in range(across):
                total = jnp.where(lane_group == b, back[b * patch : (b + 1) * patch], total)
            grads[me, q * 8 + r] = total.astype(bf)

    def block_copy(q, source, to_sky, to_depth, slot):
        block = grads.at[source, pl.ds(q * 8, 8)]
        return pltpu.make_async_remote_copy(
            src_ref=block,
            dst_ref=block,
            send_sem=send_sem.at[slot, q],
            recv_sem=recv_sem.at[source, q],
            device_id={"sky": to_sky, "depth": to_depth},
            device_id_type=MESH,
        )

    def index(a, b):
        return a * depth_count + b

    def plan():
        own, relay, last = [], [], []
        slot = 0
        for step in range(1, sky_count):
            own.append((me, lax.rem(sky + step, sky_count), depth, slot))
            slot += 1
        for step in range(1, columns):
            own.append((me, sky, lax.rem(depth + 2 * step, depth_count), slot))
            slot += 1
        own.append((me, sky, partner, slot))
        slot += 1
        for step in range(1, sky_count):
            source = index(lax.rem(sky + step, sky_count), depth)
            sends = []
            for other in range(1, columns):
                sends.append((source, sky, lax.rem(depth + 2 * other, depth_count), slot))
                slot += 1
            sends.append((source, sky, partner, slot))
            slot += 1
            relay.append((source, sends))
        for step in range(sky_count):
            for other in range(1, columns):
                source = index(
                    lax.rem(sky + step, sky_count), lax.rem(depth + 2 * other, depth_count)
                )
                last.append((source, [(source, sky, partner, slot)]))
                slot += 1
        final = [
            index(lax.rem(sky + step, sky_count), lax.rem(partner + 2 * other, depth_count))
            for step in range(sky_count)
            for other in range(columns)
        ]
        return own, relay, last, final

    own, relay, last, final = plan()

    def arrived(q, source):
        block_copy(q, source, sky, partner, 0).wait_recv()

    def forward(q, items):
        for source, sends in items:
            arrived(q, source)
            for send in sends:
                block_copy(q, *send).start()

    def mix_tables():
        for step in range(1, group):
            a, b = shifted(step // depth_count, step % depth_count)
            pltpu.make_async_remote_copy(
                src_ref=table.at[me],
                dst_ref=table.at[index(a, b)],
                send_sem=table_send.at[step],
                recv_sem=table_recv.at[index(a, b)],
                device_id={"sky": a, "depth": b},
                device_id_type=MESH,
            ).wait_recv()
        first_tile = (sky * TPD + depth * tiles_here).astype(jnp.float32)
        cells = slab[...].astype(jnp.float32)
        cell_count = cells.shape[1]
        square = jnp.broadcast_to(cells, (cell_count, cell_count))
        thickness = jnp.sum((square == square.T).astype(jnp.float32), axis=0, keepdims=True)
        wanted = jnp.concatenate(
            [cells * float(tile_count) + first_tile + float(t) for t in range(tiles_here)], axis=1
        )
        inverse = jnp.concatenate([1.0 / thickness] * tiles_here, axis=1)

        @pl.loop(0, group)
        def _(device):
            entries = table[device]
            total = jnp.zeros((patch, wanted.shape[1]), jnp.float32)
            for k in range(ov):
                hit = entries[:, k : k + 1] == wanted
                total = total + jnp.where(hit, entries[:, ov + k : ov + k + 1], 0.0)
            mixing[device] = (total * inverse).astype(bf)

    def deposit(q):
        weights = mixing[...].reshape(group * patch, -1)
        cell_count = slab.shape[1]
        for r in range(8):
            rows = grads[:, pl.ds(q * 8 + r, 1)].reshape(group * patch, width)
            made = lax.dot_general(
                rows, weights, (((0,), (0,)), ((), ())), preferred_element_type=jnp.float32
            ).astype(bf)
            for t in range(tiles_here):
                out[q * 8 + r, t * width : (t + 1) * width, :] = made[
                    :, t * cell_count : (t + 1) * cell_count
                ]

    def step_body(k, carry):
        @pl.when(k < chunks)
        def _():
            compute(k)
            for send in own:
                block_copy(k, *send).start()

        @pl.when((k >= 1) & (k < chunks + 1))
        def _():
            forward(k - 1, relay)

        @pl.when((k >= 2) & (k < chunks + 2))
        def _():
            forward(k - 2, last)

        @pl.when(k == 2)
        def _():
            mix_tables()

        @pl.when(k >= 3)
        def _():
            for source in final:
                arrived(k - 3, source)
            deposit(k - 3)

        return carry

    lax.fori_loop(0, chunks + 3, step_body, 0)

    def drain(q, carry):
        for send in own:
            block_copy(q, *send).wait_send()
        for source, sends in relay + last:
            for send in sends:
                block_copy(q, *send).wait_send()
        return carry

    lax.fori_loop(0, chunks, drain, 0)
    for step in range(1, group):
        table_copy(step).wait_send()


def body_gather(
    convergence, summary_cot, stem_w, down_w, block_w, plane_ids, tile_ids, lens_weight, slab_map
):
    sky_count, depth_count = lax.axis_size("sky"), lax.axis_size("depth")
    group = sky_count * depth_count
    patch, height, width = convergence.shape
    tiles_here = TPD // depth_count
    cells = slab_map.shape[0]
    chunks = height // 8
    operands = (
        convergence,
        summary_cot,
        stem_w,
        down_w,
        block_w,
        plane_ids,
        tile_ids,
        lens_weight,
        slab_map.reshape(1, cells),
    )
    return pl.pallas_call(
        functools.partial(pencil_kernel, (sky_count, depth_count, sky_count * TPD)),
        out_shape=jax.ShapeDtypeStruct((height, tiles_here * width, cells), jnp.bfloat16),
        in_specs=[pl.BlockSpec(memory_space=pl.ANY)] * len(operands),
        out_specs=pl.BlockSpec(memory_space=pltpu.VMEM),
        scratch_shapes=[pltpu.VMEM(x.shape, x.dtype) for x in operands]
        + [
            pltpu.SemaphoreType.DMA((len(operands),)),
            pltpu.VMEM((group, height, patch, width), jnp.bfloat16),
            pltpu.VMEM((group, patch, 128), jnp.float32),
            pltpu.VMEM((8 * width, down_w.shape[0]), jnp.bfloat16),
            pltpu.VMEM((group, patch, tiles_here * cells), jnp.bfloat16),
            pltpu.SemaphoreType.DMA((group, chunks)),
            pltpu.SemaphoreType.DMA((group, chunks)),
            pltpu.SemaphoreType.DMA((group,)),
            pltpu.SemaphoreType.DMA((group,)),
        ],
        compiler_params=pltpu.CompilerParams(
            collective_id=0, has_side_effects=True, vmem_limit_bytes=67043328
        ),
        name="pencil",
    )(*operands)


def body(convergence, summary_cot, stem_w, down_w, block_w, plane_ids, *rest):
    group = lax.axis_size("sky") * lax.axis_size("depth")
    gathered = group * convergence.shape[0]
    exchanged = 2 * plane_ids.size
    form = body_gather if gathered <= exchanged else body_exchange
    return form(convergence, summary_cot, stem_w, down_w, block_w, plane_ids, *rest)


def solution(mesh):
    placed = (
        P(("group", "sky", "depth"), None, None),
        P(("group", "sky", "depth"), None),
        P(),
        P(),
        P(),
        P(("group", "sky", "depth"), None),
        P(("group", "sky", "depth"), None),
        P(("group", "sky", "depth"), None),
        P(),
    )
    return jax.shard_map(
        body,
        mesh=mesh,
        in_specs=placed,
        out_specs=P(("group", "sky"), "depth", None),
        check_vma=False,
    )
```

```python
import functools

import jax
import jax.numpy as jnp
from jax import lax
from jax.experimental import pallas as pl
from jax.experimental.pallas import tpu as pltpu
from jax.sharding import PartitionSpec as P

PLANES = 64
TPD = 8
READY = 0


def summarize(maps, stem_w, down_w, block_w):
    patch_count, height, breadth = maps.shape
    chans_low = stem_w.shape[1]
    rounded = maps.astype(jnp.bfloat16)
    blocks_four = rounded.reshape(patch_count, height // 4, 4, breadth // 4, 4)
    stem_in = blocks_four.transpose(2, 4, 0, 1, 3).reshape(
        16, patch_count * (height // 4) * (breadth // 4)
    )
    stem_out = jax.nn.silu(jnp.dot(stem_w.T, stem_in, preferred_element_type=jnp.float32)).astype(
        jnp.bfloat16
    )
    coarse = stem_out.reshape(chans_low, patch_count, height // 8, 2, breadth // 8, 2)
    down_in = coarse.transpose(0, 3, 5, 1, 2, 4).reshape(
        4 * chans_low, patch_count * (height // 8) * (breadth // 8)
    )
    stream = jax.nn.silu(jnp.dot(down_w.T, down_in, preferred_element_type=jnp.float32))
    for layer in range(block_w.shape[0]):
        inner = jax.nn.silu(
            jnp.dot(
                block_w[layer, 0].T, stream.astype(jnp.bfloat16), preferred_element_type=jnp.float32
            )
        ).astype(jnp.bfloat16)
        stream = stream + jnp.dot(block_w[layer, 1].T, inner, preferred_element_type=jnp.float32)
    pooled = stream.reshape(stream.shape[0], patch_count, -1).sum(axis=2)
    return pooled.T


def body_exchange(
    convergence, summary_cot, stem_w, down_w, block_w, plane_ids, tile_ids, lens_weight, slab_map
):
    sky_count = lax.axis_size("sky")
    depth_count = lax.axis_size("depth")
    patch_here, height, breadth = convergence.shape
    pixels = height * breadth
    intersections = plane_ids.shape[1]
    slab_planes = PLANES // depth_count
    target_count = slab_planes * TPD
    _, pullback = jax.vjp(lambda values: summarize(values, stem_w, down_w, block_w), convergence)
    grads = pullback(summary_cot)[0].reshape(patch_here, pixels)
    target_rows = jnp.arange(target_count, dtype=jnp.int32)
    accelerator_list = sky_count * depth_count
    entries = patch_here * intersections
    capacity = max(2, 2 * entries // accelerator_list)
    weighted = (
        (lens_weight[:, :, None] * grads[:, None, :]).astype(jnp.bfloat16).reshape(entries, pixels)
    )
    flat_planes = plane_ids.reshape(-1)
    flat_tiles = tile_ids.reshape(-1)
    owner = flat_tiles // TPD * depth_count + flat_planes // slab_planes
    hits = (owner[:, None] == jnp.arange(accelerator_list, dtype=jnp.int32)[None, :]).astype(
        jnp.int32
    )
    before = jnp.sum((jnp.cumsum(hits, axis=0) - hits) * hits, axis=1)
    slot_index = owner * capacity + before
    local_slot = flat_planes % slab_planes * TPD + flat_tiles % TPD
    outgoing = (
        jnp.zeros((accelerator_list * capacity, pixels), jnp.bfloat16).at[slot_index].set(weighted)
    )
    outgoing = outgoing.reshape(sky_count, depth_count, capacity, pixels)
    out_slots = (
        jnp.full((accelerator_list * capacity,), -1, jnp.int32).at[slot_index].set(local_slot)
    )
    out_slots = out_slots.reshape(sky_count, depth_count, capacity)
    incoming, in_slots = (
        lax.all_to_all(
            lax.all_to_all(outgoing, "sky", split_axis=0, concat_axis=0, tiled=True),
            "depth",
            split_axis=1,
            concat_axis=1,
            tiled=True,
        ),
        lax.all_to_all(
            lax.all_to_all(out_slots, "sky", split_axis=0, concat_axis=0, tiled=True),
            "depth",
            split_axis=1,
            concat_axis=1,
            tiled=True,
        ),
    )
    selector = (in_slots.reshape(-1)[None, :] == target_rows[:, None]).astype(jnp.bfloat16)
    deposit = jnp.dot(selector, incoming.reshape(-1, pixels), preferred_element_type=jnp.float32)
    plane_block = (
        deposit.reshape(slab_planes, TPD, height, breadth)
        .transpose(0, 2, 1, 3)
        .reshape(slab_planes, height, TPD * breadth)
    )
    pencil_planes = lax.all_to_all(
        plane_block.astype(jnp.bfloat16), "depth", split_axis=2, concat_axis=0, tiled=True
    ).astype(plane_block.dtype)
    member = (slab_map[:, None] == jnp.arange(PLANES, dtype=jnp.int32)[None, :]).astype(jnp.float32)
    thickness = jnp.sum(member, axis=0)
    spread = member * (1.0 / thickness)[None, :]
    pencil = jnp.einsum("lxy,zl->xyz", pencil_planes, spread, precision=lax.Precision.HIGHEST)
    return pencil.astype(jnp.bfloat16)


MESH = pl.DeviceIdType.MESH


def sigmoid(v):
    return 0.5 * jnp.tanh(0.5 * v) + 0.5


def silu_pair(v):
    gate = sigmoid(v)
    value = v * gate
    return value, gate + value * (1.0 - gate)


def dot(a, b):
    return jnp.dot(a, b, preferred_element_type=jnp.float32)


def dot_t(a, b):
    return lax.dot_general(a, b, (((1,), (1,)), ((), ())), preferred_element_type=jnp.float32)


def pencil_kernel(
    sizes,
    *refs,
):
    inputs, (out, *held), rest = refs[:9], refs[9:19], refs[19:]
    load_sem, rest = rest[0], rest[1:]
    loads = [
        pltpu.make_async_copy(source, target, load_sem.at[i])
        for i, (source, target) in enumerate(zip(inputs, held))
    ]
    for i in (5, 6, 7, 2, 0, 3, 4, 1, 8):
        loads[i].start()
    pencil_steps(sizes, loads, *held, out, *rest)


def pencil_steps(
    sizes,
    loads,
    conv,
    cot,
    stem_w,
    down_w,
    block_w,
    planes,
    tiles,
    lens,
    slab,
    out,
    grads,
    taps,
    mixing,
    send_sem,
    recv_sem,
):
    sky_count, depth_count, tile_count = sizes
    bf = jnp.bfloat16
    patch, height, width = conv.shape
    low, wide = stem_w.shape[1], down_w.shape[0]
    chunks, across = height // 8, width // 8
    ov = planes.shape[1]
    tiles_here = TPD // depth_count
    group = sky_count * depth_count
    sky, depth = lax.axis_index("sky"), lax.axis_index("depth")
    core = lax.rem(depth, 2)
    partner = depth + 1 - 2 * core
    columns = depth_count // 2
    me = sky * depth_count + depth

    def shifted(by_sky, by_depth):
        return lax.rem(sky + by_sky, sky_count), lax.rem(depth + by_depth, depth_count)

    barrier = pltpu.get_barrier_semaphore()
    for step in range(1, group):
        to_sky, to_depth = shifted(step // depth_count, step % depth_count)
        pl.semaphore_signal(
            barrier, inc=1, device_id={"sky": to_sky, "depth": to_depth}, device_id_type=MESH
        )

    for i in (5, 6, 7):
        loads[i].wait()
    rough = lens[...].astype(bf)
    fine = (lens[...] - rough.astype(jnp.float32)).astype(bf)
    ids = [planes[...].astype(jnp.float32).astype(bf), tiles[...].astype(jnp.float32).astype(bf)]
    blank = jnp.zeros((patch, width - 4 * ov), bf)
    grads[me, 0] = jnp.concatenate(ids + [rough, fine, blank], axis=1)

    loads[2].wait()
    row = lax.broadcasted_iota(jnp.int32, (8 * width, patch), 0)
    tap = ((row >> (width.bit_length() - 1)) & 3) * 4 + (row & 3)
    pick = (tap == lax.broadcasted_iota(jnp.int32, (8 * width, patch), 1)).astype(bf)
    widen = (
        lax.broadcasted_iota(jnp.int32, (low, wide), 1) >> 2
        == lax.broadcasted_iota(jnp.int32, (low, wide), 0)
    ).astype(bf)
    spread = dot(pick, dot(stem_w[...], widen).astype(bf))
    row = lax.broadcasted_iota(jnp.int32, (8 * width, wide), 0)
    lane = lax.broadcasted_iota(jnp.int32, (8 * width, wide), 1)
    row_half = row >> (width.bit_length() + 1)
    same = (row_half == ((lane >> 1) & 1)) & (((row >> 2) & 1) == (lane & 1))
    taps[...] = jnp.where(same, spread, 0.0).astype(bf)

    for i in (0, 3, 4, 1, 8):
        loads[i].wait()
    lane_group = lax.broadcasted_iota(jnp.int32, (patch, width), 1) >> 3

    def compute(q):
        streams = []
        for r in range(8):
            rows = conv[:, pl.ds(q * 8 + r, 1), :].reshape(patch, width)
            streams.append(
                jnp.concatenate(
                    [jnp.where(lane_group == b, rows, 0.0).astype(bf) for b in range(across)],
                    axis=0,
                )
            )
        stem_in = jnp.concatenate(streams, axis=1)
        stem, stem_slope = silu_pair(dot(stem_in, taps[...]))
        stream, down_slope = silu_pair(dot(stem.astype(bf), down_w[...]))
        slopes = []
        for layer in range(block_w.shape[0]):
            inner, slope = silu_pair(dot(stream.astype(bf), block_w[layer, 0]))
            slopes.append(slope)
            if layer + 1 < block_w.shape[0]:
                stream = stream + dot(inner.astype(bf), block_w[layer, 1])
        flow = jnp.concatenate([cot[...]] * across, axis=0)
        for layer in reversed(range(block_w.shape[0])):
            inner = dot_t(flow.astype(bf), block_w[layer, 1]).astype(bf).astype(jnp.float32)
            inner = (inner * slopes[layer]).astype(bf)
            flow = flow + dot_t(inner, block_w[layer, 0]).astype(bf).astype(jnp.float32)
        flow = dot_t((flow * down_slope).astype(bf), down_w[...]).astype(bf).astype(jnp.float32)
        flow = (flow * stem_slope).astype(bf)
        for r in range(8):
            back = dot_t(flow, taps[pl.ds(r * width, width), :])
            total = jnp.zeros((patch, width), jnp.float32)
            for b in range(across):
                total = jnp.where(lane_group == b, back[b * patch : (b + 1) * patch], total)
            grads[me, q * 8 + r + 1] = total.astype(bf)

    def block_copy(first, q, source, to_sky, to_depth, slot):
        block = grads.at[source, pl.ds(0, 9)] if first else grads.at[source, pl.ds(q * 8 + 1, 8)]
        return pltpu.make_async_remote_copy(
            src_ref=block,
            dst_ref=block,
            send_sem=send_sem.at[slot, q],
            recv_sem=recv_sem.at[source, q],
            device_id={"sky": to_sky, "depth": to_depth},
            device_id_type=MESH,
        )

    def index(a, b):
        return a * depth_count + b

    def plan():
        own, relay, last = [], [], []
        slot = 0
        for step in range(1, sky_count):
            own.append((me, lax.rem(sky + step, sky_count), depth, slot))
            slot += 1
        for step in range(1, columns):
            own.append((me, sky, lax.rem(depth + 2 * step, depth_count), slot))
            slot += 1
        own.append((me, sky, partner, slot))
        slot += 1
        for step in range(1, sky_count):
            source = index(lax.rem(sky + step, sky_count), depth)
            sends = []
            for other in range(1, columns):
                sends.append((source, sky, lax.rem(depth + 2 * other, depth_count), slot))
                slot += 1
            sends.append((source, sky, partner, slot))
            slot += 1
            relay.append((source, sends))
        for step in range(sky_count):
            for other in range(1, columns):
                source = index(
                    lax.rem(sky + step, sky_count), lax.rem(depth + 2 * other, depth_count)
                )
                last.append((source, [(source, sky, partner, slot)]))
                slot += 1
        final = [
            index(lax.rem(sky + step, sky_count), lax.rem(partner + 2 * other, depth_count))
            for step in range(sky_count)
            for other in range(columns)
        ]
        return own, relay, last, final

    own, relay, last, final = plan()

    def arrived(first, q, source):
        block_copy(first, q, source, sky, partner, 0).wait_recv()

    def forward(first, q, items):
        for source, sends in items:
            arrived(first, q, source)
            for send in sends:
                block_copy(first, q, *send).start()

    def mix_tables():
        first_tile = (sky * TPD + depth * tiles_here).astype(jnp.float32)
        cells = slab[...].astype(jnp.float32)
        cell_count = cells.shape[1]
        square = jnp.broadcast_to(cells, (cell_count, cell_count))
        thickness = jnp.sum((square == square.T).astype(jnp.float32), axis=0, keepdims=True)
        wanted = jnp.concatenate(
            [cells * float(tile_count) + first_tile + float(t) for t in range(tiles_here)], axis=1
        )
        inverse = jnp.concatenate([1.0 / thickness] * tiles_here, axis=1)

        @pl.loop(0, group, unroll=4)
        def _(device):
            entries = grads[device, 0].astype(jnp.float32)
            code = entries[:, 0:ov] * float(tile_count) + entries[:, ov : 2 * ov]
            weight = entries[:, 2 * ov : 3 * ov] + entries[:, 3 * ov : 4 * ov]
            total = jnp.zeros((patch, wanted.shape[1]), jnp.float32)
            for k in range(ov):
                hit = code[:, k : k + 1] == wanted
                total = total + jnp.where(hit, weight[:, k : k + 1], 0.0)
            mixing[device] = (total * inverse).astype(bf)

    def deposit(q):
        weights = mixing[...].reshape(group * patch, -1)
        cell_count = slab.shape[1]
        for r in range(8):
            rows = grads[:, pl.ds(q * 8 + r + 1, 1)].reshape(group * patch, width)
            made = lax.dot_general(
                rows, weights, (((0,), (0,)), ((), ())), preferred_element_type=jnp.float32
            ).astype(bf)
            for t in range(tiles_here):
                out[q * 8 + r, t * width : (t + 1) * width, :] = made[
                    :, t * cell_count : (t + 1) * cell_count
                ]

    def send_own(first, q):
        for send in own:
            block_copy(first, q, *send).start()

    def compute_step(k, carry):
        compute(k)

        @pl.when(k == READY)
        def _():
            pl.semaphore_wait(barrier, group - 1)
            send_own(True, 0)
            for q in range(1, READY + 1):
                send_own(False, q)

        @pl.when(k > READY)
        def _():
            send_own(False, k)

        return carry

    lax.fori_loop(0, chunks, compute_step, 0)
    for q in range(chunks):
        forward(q == 0, q, relay)
        if q > 0:
            forward(q == 1, q - 1, last)
    for q in range(chunks):
        if q == chunks - 2:
            forward(False, chunks - 1, last)
        for source in final:
            arrived(q == 0, q, source)
        if q == 0:
            mix_tables()
        deposit(q)
    for q in range(chunks):
        for send in own:
            block_copy(q == 0, q, *send).wait_send()
        for source, sends in relay + last:
            for send in sends:
                block_copy(q == 0, q, *send).wait_send()


def body_gather(
    convergence, summary_cot, stem_w, down_w, block_w, plane_ids, tile_ids, lens_weight, slab_map
):
    sky_count, depth_count = lax.axis_size("sky"), lax.axis_size("depth")
    group = sky_count * depth_count
    patch, height, width = convergence.shape
    tiles_here = TPD // depth_count
    cells = slab_map.shape[0]
    chunks = height // 8
    operands = (
        convergence,
        summary_cot,
        stem_w,
        down_w,
        block_w,
        plane_ids,
        tile_ids,
        lens_weight,
        slab_map.reshape(1, cells),
    )
    return pl.pallas_call(
        functools.partial(pencil_kernel, (sky_count, depth_count, sky_count * TPD)),
        out_shape=jax.ShapeDtypeStruct((height, tiles_here * width, cells), jnp.bfloat16),
        in_specs=[pl.BlockSpec(memory_space=pl.ANY)] * len(operands),
        out_specs=pl.BlockSpec(memory_space=pltpu.VMEM),
        scratch_shapes=[pltpu.VMEM(x.shape, x.dtype) for x in operands]
        + [
            pltpu.SemaphoreType.DMA((len(operands),)),
            pltpu.VMEM((group, height + 1, patch, width), jnp.bfloat16),
            pltpu.VMEM((8 * width, down_w.shape[0]), jnp.bfloat16),
            pltpu.VMEM((group, patch, tiles_here * cells), jnp.bfloat16),
            pltpu.SemaphoreType.DMA((group, chunks)),
            pltpu.SemaphoreType.DMA((group, chunks)),
        ],
        compiler_params=pltpu.CompilerParams(
            collective_id=0, has_side_effects=True, vmem_limit_bytes=67043328
        ),
        name="pencil",
    )(*operands)


def body(convergence, summary_cot, stem_w, down_w, block_w, plane_ids, *rest):
    group = lax.axis_size("sky") * lax.axis_size("depth")
    gathered = group * convergence.shape[0]
    exchanged = 2 * plane_ids.size
    form = body_gather if gathered <= exchanged else body_exchange
    return form(convergence, summary_cot, stem_w, down_w, block_w, plane_ids, *rest)


def solution(mesh):
    placed = (
        P(("group", "sky", "depth"), None, None),
        P(("group", "sky", "depth"), None),
        P(),
        P(),
        P(),
        P(("group", "sky", "depth"), None),
        P(("group", "sky", "depth"), None),
        P(("group", "sky", "depth"), None),
        P(),
    )
    return jax.shard_map(
        body,
        mesh=mesh,
        in_specs=placed,
        out_specs=P(("group", "sky"), "depth", None),
        check_vma=False,
    )
```

```python
import functools

import jax
import jax.numpy as jnp
from jax import lax
from jax.experimental import pallas as pl
from jax.experimental.pallas import tpu as pltpu
from jax.sharding import PartitionSpec as P

PLANES = 64
TPD = 8
READY = 0
LAG = 2


def summarize(maps, stem_w, down_w, block_w):
    patch_count, height, breadth = maps.shape
    chans_low = stem_w.shape[1]
    rounded = maps.astype(jnp.bfloat16)
    blocks_four = rounded.reshape(patch_count, height // 4, 4, breadth // 4, 4)
    stem_in = blocks_four.transpose(2, 4, 0, 1, 3).reshape(
        16, patch_count * (height // 4) * (breadth // 4)
    )
    stem_out = jax.nn.silu(jnp.dot(stem_w.T, stem_in, preferred_element_type=jnp.float32)).astype(
        jnp.bfloat16
    )
    coarse = stem_out.reshape(chans_low, patch_count, height // 8, 2, breadth // 8, 2)
    down_in = coarse.transpose(0, 3, 5, 1, 2, 4).reshape(
        4 * chans_low, patch_count * (height // 8) * (breadth // 8)
    )
    stream = jax.nn.silu(jnp.dot(down_w.T, down_in, preferred_element_type=jnp.float32))
    for layer in range(block_w.shape[0]):
        inner = jax.nn.silu(
            jnp.dot(
                block_w[layer, 0].T, stream.astype(jnp.bfloat16), preferred_element_type=jnp.float32
            )
        ).astype(jnp.bfloat16)
        stream = stream + jnp.dot(block_w[layer, 1].T, inner, preferred_element_type=jnp.float32)
    pooled = stream.reshape(stream.shape[0], patch_count, -1).sum(axis=2)
    return pooled.T


def body_exchange(
    convergence, summary_cot, stem_w, down_w, block_w, plane_ids, tile_ids, lens_weight, slab_map
):
    sky_count = lax.axis_size("sky")
    depth_count = lax.axis_size("depth")
    patch_here, height, breadth = convergence.shape
    pixels = height * breadth
    intersections = plane_ids.shape[1]
    slab_planes = PLANES // depth_count
    target_count = slab_planes * TPD
    _, pullback = jax.vjp(lambda values: summarize(values, stem_w, down_w, block_w), convergence)
    grads = pullback(summary_cot)[0].reshape(patch_here, pixels)
    target_rows = jnp.arange(target_count, dtype=jnp.int32)
    accelerator_list = sky_count * depth_count
    entries = patch_here * intersections
    capacity = max(2, 2 * entries // accelerator_list)
    weighted = (
        (lens_weight[:, :, None] * grads[:, None, :]).astype(jnp.bfloat16).reshape(entries, pixels)
    )
    flat_planes = plane_ids.reshape(-1)
    flat_tiles = tile_ids.reshape(-1)
    owner = flat_tiles // TPD * depth_count + flat_planes // slab_planes
    hits = (owner[:, None] == jnp.arange(accelerator_list, dtype=jnp.int32)[None, :]).astype(
        jnp.int32
    )
    before = jnp.sum((jnp.cumsum(hits, axis=0) - hits) * hits, axis=1)
    slot_index = owner * capacity + before
    local_slot = flat_planes % slab_planes * TPD + flat_tiles % TPD
    outgoing = (
        jnp.zeros((accelerator_list * capacity, pixels), jnp.bfloat16).at[slot_index].set(weighted)
    )
    outgoing = outgoing.reshape(sky_count, depth_count, capacity, pixels)
    out_slots = (
        jnp.full((accelerator_list * capacity,), -1, jnp.int32).at[slot_index].set(local_slot)
    )
    out_slots = out_slots.reshape(sky_count, depth_count, capacity)
    incoming, in_slots = (
        lax.all_to_all(
            lax.all_to_all(outgoing, "sky", split_axis=0, concat_axis=0, tiled=True),
            "depth",
            split_axis=1,
            concat_axis=1,
            tiled=True,
        ),
        lax.all_to_all(
            lax.all_to_all(out_slots, "sky", split_axis=0, concat_axis=0, tiled=True),
            "depth",
            split_axis=1,
            concat_axis=1,
            tiled=True,
        ),
    )
    selector = (in_slots.reshape(-1)[None, :] == target_rows[:, None]).astype(jnp.bfloat16)
    deposit = jnp.dot(selector, incoming.reshape(-1, pixels), preferred_element_type=jnp.float32)
    plane_block = (
        deposit.reshape(slab_planes, TPD, height, breadth)
        .transpose(0, 2, 1, 3)
        .reshape(slab_planes, height, TPD * breadth)
    )
    pencil_planes = lax.all_to_all(
        plane_block.astype(jnp.bfloat16), "depth", split_axis=2, concat_axis=0, tiled=True
    ).astype(plane_block.dtype)
    member = (slab_map[:, None] == jnp.arange(PLANES, dtype=jnp.int32)[None, :]).astype(jnp.float32)
    thickness = jnp.sum(member, axis=0)
    spread = member * (1.0 / thickness)[None, :]
    pencil = jnp.einsum("lxy,zl->xyz", pencil_planes, spread, precision=lax.Precision.HIGHEST)
    return pencil.astype(jnp.bfloat16)


MESH = pl.DeviceIdType.MESH


def sigmoid(v):
    return 0.5 * jnp.tanh(0.5 * v) + 0.5


def silu_pair(v):
    gate = sigmoid(v)
    value = v * gate
    return value, gate + value * (1.0 - gate)


def dot(a, b):
    return jnp.dot(a, b, preferred_element_type=jnp.float32)


def dot_t(a, b):
    return lax.dot_general(a, b, (((1,), (1,)), ((), ())), preferred_element_type=jnp.float32)


def pencil_kernel(
    sizes,
    *refs,
):
    inputs, (out, *held), rest = refs[:9], refs[9:19], refs[19:]
    load_sem, rest = rest[0], rest[1:]
    loads = [
        pltpu.make_async_copy(source, target, load_sem.at[i])
        for i, (source, target) in enumerate(zip(inputs, held))
    ]
    for i in (5, 6, 7, 2, 0, 3, 4, 1, 8):
        loads[i].start()
    pencil_steps(sizes, loads, *held, out, *rest)


def pencil_steps(
    sizes,
    loads,
    conv,
    cot,
    stem_w,
    down_w,
    block_w,
    planes,
    tiles,
    lens,
    slab,
    out,
    grads,
    taps,
    mixing,
    send_sem,
    recv_sem,
):
    sky_count, depth_count, tile_count = sizes
    bf = jnp.bfloat16
    patch, height, width = conv.shape
    low, wide = stem_w.shape[1], down_w.shape[0]
    chunks, across = height // 8, width // 8
    ov = planes.shape[1]
    tiles_here = TPD // depth_count
    group = sky_count * depth_count
    sky, depth = lax.axis_index("sky"), lax.axis_index("depth")
    core = lax.rem(depth, 2)
    partner = depth + 1 - 2 * core
    columns = depth_count // 2
    me = sky * depth_count + depth

    def shifted(by_sky, by_depth):
        return lax.rem(sky + by_sky, sky_count), lax.rem(depth + by_depth, depth_count)

    barrier = pltpu.get_barrier_semaphore()
    for step in range(1, group):
        to_sky, to_depth = shifted(step // depth_count, step % depth_count)
        pl.semaphore_signal(
            barrier, inc=1, device_id={"sky": to_sky, "depth": to_depth}, device_id_type=MESH
        )

    for i in (5, 6, 7):
        loads[i].wait()
    rough = lens[...].astype(bf)
    fine = (lens[...] - rough.astype(jnp.float32)).astype(bf)
    ids = [planes[...].astype(jnp.float32).astype(bf), tiles[...].astype(jnp.float32).astype(bf)]
    blank = jnp.zeros((patch, width - 4 * ov), bf)
    grads[me, 0] = jnp.concatenate(ids + [rough, fine, blank], axis=1)

    loads[2].wait()
    row = lax.broadcasted_iota(jnp.int32, (8 * width, patch), 0)
    tap = ((row >> (width.bit_length() - 1)) & 3) * 4 + (row & 3)
    pick = (tap == lax.broadcasted_iota(jnp.int32, (8 * width, patch), 1)).astype(bf)
    widen = (
        lax.broadcasted_iota(jnp.int32, (low, wide), 1) >> 2
        == lax.broadcasted_iota(jnp.int32, (low, wide), 0)
    ).astype(bf)
    spread = dot(pick, dot(stem_w[...], widen).astype(bf))
    row = lax.broadcasted_iota(jnp.int32, (8 * width, wide), 0)
    lane = lax.broadcasted_iota(jnp.int32, (8 * width, wide), 1)
    row_half = row >> (width.bit_length() + 1)
    same = (row_half == ((lane >> 1) & 1)) & (((row >> 2) & 1) == (lane & 1))
    taps[...] = jnp.where(same, spread, 0.0).astype(bf)

    for i in (0, 3, 4, 1, 8):
        loads[i].wait()
    lane_group = lax.broadcasted_iota(jnp.int32, (patch, width), 1) >> 3

    def compute(q):
        streams = []
        for r in range(8):
            rows = conv[:, pl.ds(q * 8 + r, 1), :].reshape(patch, width)
            streams.append(
                jnp.concatenate(
                    [jnp.where(lane_group == b, rows, 0.0).astype(bf) for b in range(across)],
                    axis=0,
                )
            )
        stem_in = jnp.concatenate(streams, axis=1)
        stem, stem_slope = silu_pair(dot(stem_in, taps[...]))
        stream, down_slope = silu_pair(dot(stem.astype(bf), down_w[...]))
        slopes = []
        for layer in range(block_w.shape[0]):
            inner, slope = silu_pair(dot(stream.astype(bf), block_w[layer, 0]))
            slopes.append(slope)
            if layer + 1 < block_w.shape[0]:
                stream = stream + dot(inner.astype(bf), block_w[layer, 1])
        flow = jnp.concatenate([cot[...]] * across, axis=0)
        for layer in reversed(range(block_w.shape[0])):
            inner = dot_t(flow.astype(bf), block_w[layer, 1]).astype(bf).astype(jnp.float32)
            inner = (inner * slopes[layer]).astype(bf)
            flow = flow + dot_t(inner, block_w[layer, 0]).astype(bf).astype(jnp.float32)
        flow = dot_t((flow * down_slope).astype(bf), down_w[...]).astype(bf).astype(jnp.float32)
        flow = (flow * stem_slope).astype(bf)
        for r in range(8):
            back = dot_t(flow, taps[pl.ds(r * width, width), :])
            total = jnp.zeros((patch, width), jnp.float32)
            for b in range(across):
                total = jnp.where(lane_group == b, back[b * patch : (b + 1) * patch], total)
            grads[me, q * 8 + r + 1] = total.astype(bf)

    def block_copy(first, q, source, to_sky, to_depth, slot):
        block = grads.at[source, pl.ds(0, 9)] if first else grads.at[source, pl.ds(q * 8 + 1, 8)]
        return pltpu.make_async_remote_copy(
            src_ref=block,
            dst_ref=block,
            send_sem=send_sem.at[slot, q],
            recv_sem=recv_sem.at[source, q],
            device_id={"sky": to_sky, "depth": to_depth},
            device_id_type=MESH,
        )

    def index(a, b):
        return a * depth_count + b

    def plan():
        own, relay, last = [], [], []
        slot = 0
        for step in range(1, sky_count):
            own.append((me, lax.rem(sky + step, sky_count), depth, slot))
            slot += 1
        for step in range(1, columns):
            own.append((me, sky, lax.rem(depth + 2 * step, depth_count), slot))
            slot += 1
        own.append((me, sky, partner, slot))
        slot += 1
        for step in range(1, sky_count):
            source = index(lax.rem(sky + step, sky_count), depth)
            sends = []
            for other in range(1, columns):
                sends.append((source, sky, lax.rem(depth + 2 * other, depth_count), slot))
                slot += 1
            sends.append((source, sky, partner, slot))
            slot += 1
            relay.append((source, sends))
        for step in range(sky_count):
            for other in range(1, columns):
                source = index(
                    lax.rem(sky + step, sky_count), lax.rem(depth + 2 * other, depth_count)
                )
                last.append((source, [(source, sky, partner, slot)]))
                slot += 1
        final = [
            index(lax.rem(sky + step, sky_count), lax.rem(partner + 2 * other, depth_count))
            for step in range(sky_count)
            for other in range(columns)
        ]
        return own, relay, last, final

    own, relay, last, final = plan()

    def arrived(first, q, source):
        block_copy(first, q, source, sky, partner, 0).wait_recv()

    def forward(first, q, items):
        for source, sends in items:
            arrived(first, q, source)
            for send in sends:
                block_copy(first, q, *send).start()

    def mix_tables():
        first_tile = (sky * TPD + depth * tiles_here).astype(jnp.float32)
        cells = slab[...].astype(jnp.float32)
        cell_count = cells.shape[1]
        square = jnp.broadcast_to(cells, (cell_count, cell_count))
        thickness = jnp.sum((square == square.T).astype(jnp.float32), axis=0, keepdims=True)
        wanted = jnp.concatenate(
            [cells * float(tile_count) + first_tile + float(t) for t in range(tiles_here)], axis=1
        )
        inverse = jnp.concatenate([1.0 / thickness] * tiles_here, axis=1)

        @pl.loop(0, group, unroll=4)
        def _(device):
            entries = grads[device, 0].astype(jnp.float32)
            code = entries[:, 0:ov] * float(tile_count) + entries[:, ov : 2 * ov]
            weight = entries[:, 2 * ov : 3 * ov] + entries[:, 3 * ov : 4 * ov]
            total = jnp.zeros((patch, wanted.shape[1]), jnp.float32)
            for k in range(ov):
                hit = code[:, k : k + 1] == wanted
                total = total + jnp.where(hit, weight[:, k : k + 1], 0.0)
            mixing[device] = (total * inverse).astype(bf)

    def deposit(q):
        weights = mixing[...].reshape(group * patch, -1)
        cell_count = slab.shape[1]
        for r in range(8):
            rows = grads[:, pl.ds(q * 8 + r + 1, 1)].reshape(group * patch, width)
            made = lax.dot_general(
                rows, weights, (((0,), (0,)), ((), ())), preferred_element_type=jnp.float32
            ).astype(bf)
            for t in range(tiles_here):
                out[q * 8 + r, t * width : (t + 1) * width, :] = made[
                    :, t * cell_count : (t + 1) * cell_count
                ]

    def send_own(first, q):
        for send in own:
            block_copy(first, q, *send).start()

    def compute_step(k, carry):
        compute(k)

        @pl.when(k == READY)
        def _():
            pl.semaphore_wait(barrier, group - 1)
            send_own(True, 0)
            for q in range(1, READY + 1):
                send_own(False, q)

        @pl.when(k > READY)
        def _():
            send_own(False, k)

        for q in range(chunks - LAG):

            @pl.when(k == q + LAG)
            def _():
                relay_step(q)

        return carry

    def relay_step(q):
        forward(q == 0, q, relay)
        if q > 0:
            forward(q == 1, q - 1, last)

    lax.fori_loop(0, chunks, compute_step, 0)
    for q in range(chunks - LAG, chunks):
        relay_step(q)
    for q in range(chunks):
        if q == chunks - 2:
            forward(False, chunks - 1, last)
        for source in final:
            arrived(q == 0, q, source)
        if q == 0:
            mix_tables()
        deposit(q)
    for q in range(chunks):
        for send in own:
            block_copy(q == 0, q, *send).wait_send()
        for source, sends in relay + last:
            for send in sends:
                block_copy(q == 0, q, *send).wait_send()


def body_gather(
    convergence, summary_cot, stem_w, down_w, block_w, plane_ids, tile_ids, lens_weight, slab_map
):
    sky_count, depth_count = lax.axis_size("sky"), lax.axis_size("depth")
    group = sky_count * depth_count
    patch, height, width = convergence.shape
    tiles_here = TPD // depth_count
    cells = slab_map.shape[0]
    chunks = height // 8
    operands = (
        convergence,
        summary_cot,
        stem_w,
        down_w,
        block_w,
        plane_ids,
        tile_ids,
        lens_weight,
        slab_map.reshape(1, cells),
    )
    return pl.pallas_call(
        functools.partial(pencil_kernel, (sky_count, depth_count, sky_count * TPD)),
        out_shape=jax.ShapeDtypeStruct((height, tiles_here * width, cells), jnp.bfloat16),
        in_specs=[pl.BlockSpec(memory_space=pl.ANY)] * len(operands),
        out_specs=pl.BlockSpec(memory_space=pltpu.VMEM),
        scratch_shapes=[pltpu.VMEM(x.shape, x.dtype) for x in operands]
        + [
            pltpu.SemaphoreType.DMA((len(operands),)),
            pltpu.VMEM((group, height + 1, patch, width), jnp.bfloat16),
            pltpu.VMEM((8 * width, down_w.shape[0]), jnp.bfloat16),
            pltpu.VMEM((group, patch, tiles_here * cells), jnp.bfloat16),
            pltpu.SemaphoreType.DMA((group, chunks)),
            pltpu.SemaphoreType.DMA((group, chunks)),
        ],
        compiler_params=pltpu.CompilerParams(
            collective_id=0, has_side_effects=True, vmem_limit_bytes=67043328
        ),
        name="pencil",
    )(*operands)


def body(convergence, summary_cot, stem_w, down_w, block_w, plane_ids, *rest):
    group = lax.axis_size("sky") * lax.axis_size("depth")
    gathered = group * convergence.shape[0]
    exchanged = 2 * plane_ids.size
    form = body_gather if gathered <= exchanged else body_exchange
    return form(convergence, summary_cot, stem_w, down_w, block_w, plane_ids, *rest)


def solution(mesh):
    placed = (
        P(("group", "sky", "depth"), None, None),
        P(("group", "sky", "depth"), None),
        P(),
        P(),
        P(),
        P(("group", "sky", "depth"), None),
        P(("group", "sky", "depth"), None),
        P(("group", "sky", "depth"), None),
        P(),
    )
    return jax.shard_map(
        body,
        mesh=mesh,
        in_specs=placed,
        out_specs=P(("group", "sky"), "depth", None),
        check_vma=False,
    )
```
